256 devices in a mesh: fsdp: 16 (over x, z_lo, core), replica: 16 (over y, z_hi).
Axes of the slice: x: 4, y: 4, z: 8 (z_hi: 4, z_lo: 2; z = z_hi * 2 + z_lo), core: 2. Of those that a mesh axis runs over, the one named last changes fastest.
Arguments:
- weights: float32 [256, 512, 2048], P('replica', 'fsdp'), may hold values from -0.125 to 0.125
- momentum: bfloat16 [256, 512, 2048], P('replica', 'fsdp'), may hold values from -6 to 6
- tokens: bfloat16 [229376, 2048], P(('fsdp', 'replica')), may hold values from -6 to 6
- block_expert: int32 [1792], P(('fsdp', 'replica')), may hold values from 0 to 255, as said below
- owner_expert: int32 [256], replicated, may hold values from 0 to 255, as said below
Outputs:
- fresh: bfloat16 [256, 512, 2048], P(('fsdp', 'replica'))
- rollout: bfloat16 [229376, 512], P(('fsdp', 'replica'))
The draws below stay inside these ranges and needn't reach their ends.
Inputs may be any that keep to these rules, and one draw needn't show every extreme that they name: `owner_expert`: within each group g the entries g * N to g * N + N - 1 (N the fsdp axis size) are a permutation of the expert numbers g * N to g * N + N - 1. `block_expert`: the blocks of the device at fsdp index f and replica index r are blocks (f * R + r) * 7 to (f * R + r) * 7 + 7 - 1 (R the replica axis size). Each names an expert that owner_expert assigns to fsdp index f; the 7 blocks of one device name experts of distinct groups; in every fsdp index one group is named by every device of that index.
All inputs are finite; a program needn't handle non-finite values.
Results may differ from the reference program's by a relative error of at most 0.008.
Values may be sent and summed in bfloat16 or wider, within the bound.
A program may use at most 128 MiB of HBM per device.

```python
import math
import jax
import jax.numpy as jnp
from jax import lax

ROWS_E = 512
COLS = 2048
ITERS = 4
BLOCKS = 7
TOK_BLOCK = 128
EXPERTS = 256
ROLL = 229376
NBLOCK = 1792
N_FSDP = 16
N_REPLICA = 16


def owner_table(key):
    keys = jax.random.split(jax.random.fold_in(key, 11), N_REPLICA)
    perms = jax.vmap(lambda k: jax.random.permutation(k, N_FSDP))(keys)
    offsets = N_FSDP * jnp.arange(N_REPLICA, dtype=jnp.int32)[:, None]
    return (perms.astype(jnp.int32) + offsets).reshape(-1).astype(jnp.int32)


def draw_owner_expert(key, part):
    return owner_table(key)


def draw_block_expert(key, part):
    table = owner_table(key).reshape(N_REPLICA, N_FSDP)
    base = jax.random.fold_in(key, 23)
    hottest = jax.random.randint(jax.random.fold_in(base, 1), (N_FSDP,), 0, N_REPLICA)

    def single(device):
        column = device // N_REPLICA
        dev_key = jax.random.fold_in(base, device + 2)
        favored = hottest[column]
        others = (favored + 1 + jax.random.permutation(jax.random.fold_in(dev_key, 1), N_REPLICA - 1)) % N_REPLICA
        chosen = jnp.concatenate([favored[None], others[:BLOCKS - 1]])
        chosen = chosen[jax.random.permutation(jax.random.fold_in(dev_key, 2), BLOCKS)]
        return table[chosen, column]
    devices = jnp.arange(N_FSDP * N_REPLICA, dtype=jnp.int32)
    return jax.vmap(single)(devices).reshape(-1).astype(jnp.int32)


def draw_momentum(key, part):
    keys = jax.random.split(jax.random.fold_in(key, 31), 3)
    noise = jnp.clip(jax.random.normal(keys[0], (EXPERTS, ROWS_E, COLS), jnp.float32), -4.0, 4.0)
    row_scale = jnp.exp(jax.random.uniform(keys[1], (EXPERTS, ROWS_E, 1), jnp.float32) * math.log(10.0))
    col_scale = jnp.exp(jax.random.uniform(keys[2], (EXPERTS, 1, COLS), jnp.float32) * math.log(10.0))
    return (0.01 * noise * row_scale * col_scale).astype(jnp.bfloat16)


def block_levels(own_key, shape, pieces, low, largest):
    def one(dim, parts):
        steps = jax.random.uniform(jax.random.fold_in(jax.random.fold_in(own_key, 6), dim), (parts,), jnp.float32, low / len(pieces), largest / len(pieces))
        return jnp.repeat(jnp.exp(steps), shape[dim] // parts).reshape((-1,) + (1,) * (len(shape) - dim - 1))

    factor_of = one(*pieces[0])
    for cut in pieces[1:]:
        factor_of = factor_of * one(*cut)
    return factor_of


def normal_values(rng, extent, deviation, most, pieces=(), kind=jnp.bfloat16):
    result = deviation * jax.random.normal(rng, extent, jnp.float32)
    if pieces:
        result = result * block_levels(rng, extent, pieces, -0.22, 0.18)
    return jnp.clip(result, -most, most).astype(kind)


def setup_inputs(seed: int = 0) -> dict:
    streams_of = jax.random.split(jax.random.key(seed), 6)
    weights = normal_values(streams_of[0], (EXPERTS, ROWS_E, COLS), COLS ** -0.5, 0.125, ((0, 16), (1, 16)), jnp.float32)
    momentum = draw_momentum(jax.random.fold_in(streams_of[5], 71), 0)
    tokens = normal_values(streams_of[2], (ROLL, COLS), 1.0, 6.0, ((0, 256),))
    block_expert = draw_block_expert(jax.random.fold_in(streams_of[5], 71), 0)
    owner_expert = draw_owner_expert(jax.random.fold_in(streams_of[5], 71), 0)
    return {"weights": weights, "momentum": momentum, "tokens": tokens, "block_expert": block_expert, "owner_expert": owner_expert}


quintic_one = 3.4445
quintic_two = -4.775
quintic_three = 2.0315
learn_rate = 0.05
weight_decay = 0.1
norm_eps = 1e-07

def orthogonalize(moment):
    wide = moment.astype(jnp.float32)
    state = (wide / (jnp.sqrt(jnp.sum(wide * wide)) + norm_eps)).astype(jnp.bfloat16)
    for _ in range(ITERS):
        current = state.astype(jnp.float32)
        square = jnp.dot(current, current.T, precision=lax.Precision.HIGHEST).astype(jnp.bfloat16)
        sq_wide = square.astype(jnp.float32)
        poly = (quintic_two * sq_wide + quintic_three * jnp.dot(sq_wide, sq_wide, precision=lax.Precision.HIGHEST)).astype(jnp.bfloat16)
        state = (quintic_one * current + jnp.dot(poly.astype(jnp.float32), current, precision=lax.Precision.HIGHEST)).astype(jnp.bfloat16)
    return state

def reference(weights, momentum, tokens, block_expert, owner_expert):
    factor = learn_rate * 0.2 * math.sqrt(max(ROWS_E, COLS))

    def refresh(index):
        update = orthogonalize(momentum[index]).astype(jnp.float32)
        return (weights[index] * (1.0 - learn_rate * weight_decay) - factor * update).astype(jnp.bfloat16)
    new_weight = lax.map(refresh, jnp.arange(EXPERTS, dtype=jnp.int32))
    slots = jnp.arange(EXPERTS, dtype=jnp.int32)
    fsdp_pos = slots // N_REPLICA
    rep_pos = slots % N_REPLICA
    order = owner_expert[rep_pos * N_FSDP + fsdp_pos]
    fresh = new_weight[order]
    blocks = tokens.reshape(NBLOCK, TOK_BLOCK, COLS)

    def serve(pair):
        rows, expert = pair
        matrix = new_weight[expert].astype(jnp.float32)
        return jnp.dot(rows.astype(jnp.float32), matrix.T, precision=lax.Precision.HIGHEST).astype(jnp.bfloat16)
    rollout = lax.map(serve, (blocks, block_expert)).reshape(ROLL, ROWS_E)
    return (fresh, rollout)
```

```python
import math

import jax
import jax.numpy as jnp
from jax import lax
from jax.sharding import PartitionSpec as P

ITERS = 4
Z_PARTS = 4


quintic_one = 3.4445
quintic_two = -4.775
quintic_three = 2.0315
learn_rate = 0.05
weight_decay = 0.1
norm_eps = 1e-07


def orthogonalize(moment):
    wide = moment.astype(jnp.float32)
    state = (wide / (jnp.sqrt(jnp.sum(wide * wide)) + norm_eps)).astype(jnp.bfloat16)
    for _ in range(ITERS):
        square = lax.dot_general(
            state, state, (((1,), (1,)), ((), ())), preferred_element_type=jnp.float32
        ).astype(jnp.bfloat16)
        twice = jnp.dot(square, square, preferred_element_type=jnp.float32)
        poly = (quintic_two * square.astype(jnp.float32) + quintic_three * twice).astype(
            jnp.bfloat16
        )
        state = (
            quintic_one * state.astype(jnp.float32)
            + jnp.dot(poly, state, preferred_element_type=jnp.float32)
        ).astype(jnp.bfloat16)
    return state


def finish(master, update):
    rows, cols = master.shape
    factor = learn_rate * 0.2 * math.sqrt(max(rows, cols))
    return (
        master.astype(jnp.float32) * (1.0 - learn_rate * weight_decay)
        - factor * update.astype(jnp.float32)
    ).astype(jnp.bfloat16)


def per_device(weights, momentum, tokens, block_expert, owner_expert):
    owners = lax.axis_size("fsdp")
    groups = lax.axis_size("replica")
    y_parts = groups // Z_PARTS
    z_groups = [[y * Z_PARTS + z for z in range(Z_PARTS)] for y in range(y_parts)]
    y_groups = [[y * Z_PARTS + z for y in range(y_parts)] for z in range(Z_PARTS)]
    group = lax.axis_index("replica")
    table = lax.dynamic_slice_in_dim(owner_expert, group * owners, owners, 0)
    local = table - group * owners
    sent_moment = momentum.at[local].get(mode="promise_in_bounds")
    whole_moment = lax.all_to_all(sent_moment, "fsdp", split_axis=0, concat_axis=1, tiled=True)
    sent_master = weights.astype(jnp.bfloat16).at[local].get(mode="promise_in_bounds")
    whole_master = lax.all_to_all(sent_master, "fsdp", split_axis=0, concat_axis=1, tiled=True)

    blocks = block_expert.shape[0]
    width = tokens.shape[1]
    resident = tokens.reshape(blocks, -1, width)
    height = resident.shape[1]
    target = block_expert // owners
    chosen = target[None, :] == jnp.arange(groups, dtype=jnp.int32)[:, None]
    source = jnp.sum(
        jnp.where(chosen, jnp.arange(blocks, dtype=jnp.int32)[None, :], 0), axis=1
    )
    outgoing = resident.at[source].get(mode="promise_in_bounds")
    outgoing = outgoing.reshape(y_parts, Z_PARTS, height, width)
    incoming = lax.all_to_all(
        outgoing, "replica", split_axis=0, concat_axis=0, tiled=True, axis_index_groups=y_groups
    )

    update = orthogonalize(whole_moment[0])
    refreshed = finish(whole_master[0], update)
    fresh = refreshed[None]
    near = lax.all_gather(refreshed, "replica", axis_index_groups=z_groups)
    product = jnp.einsum(
        "yzrd,zod->yzro", incoming, near, preferred_element_type=jnp.float32
    ).astype(jnp.bfloat16)
    answers = lax.all_to_all(
        product, "replica", split_axis=0, concat_axis=0, tiled=True, axis_index_groups=y_groups
    )
    answers = answers.reshape(groups, height, -1)
    rollout = answers.at[target].get(mode="promise_in_bounds").reshape(blocks * height, -1)
    return (fresh, rollout)


def solution(mesh):
    placed = (
        P("replica", "fsdp", None),
        P("replica", "fsdp", None),
        P(("fsdp", "replica"), None),
        P(("fsdp", "replica")),
        P(),
    )
    return jax.shard_map(
        per_device,
        mesh=mesh,
        in_specs=placed,
        out_specs=(P(("fsdp", "replica"), None, None), P(("fsdp", "replica"), None)),
        check_vma=False,
    )
```

```python
import math

import jax
import jax.numpy as jnp
from jax import lax
from jax.experimental import pallas as pl
from jax.experimental.pallas import tpu as pltpu
from jax.sharding import PartitionSpec as P

ITERS = 4
Z_PARTS = 4
PIECES = 8
TILE = 256
MESH = pl.DeviceIdType.MESH

quintic_one = 3.4445
quintic_two = -4.775
quintic_three = 2.0315
learn_rate = 0.05
weight_decay = 0.1
norm_eps = 1e-07


def dot(left, right, transposed=False):
    dims = (((1,), (1 if transposed else 0,)), ((), ()))
    return lax.dot_general(left, right, dims, preferred_element_type=jnp.float32)


def kernel(
    block_ref,
    owner_ref,
    weights,
    momentum,
    tokens,
    fresh,
    rollout,
    mom_in,
    mas_in,
    tok_in,
    mom_out,
    mas_out,
    state,
    master,
    tok_out,
    tok_all,
    mats,
    square,
    poly,
    ans_out,
    answers,
    result,
    load_sem,
    mom_send,
    mom_recv,
    mas_send,
    mas_recv,
    tok_send,
    tok_recv,
    own_send,
    own_recv,
    fwd_send,
    fwd_recv,
    ans_send,
    ans_recv,
    store_sem,
):
    owners = lax.axis_size("fsdp")
    groups = lax.axis_size("replica")
    y_parts = groups // Z_PARTS
    rows, cols = state.shape
    shard = rows // owners
    blocks, height, _ = tok_in.shape
    f = lax.axis_index("fsdp")
    r = lax.axis_index("replica")
    y = r // Z_PARTS
    q = r - y * Z_PARTS
    left = lax.rem(q + Z_PARTS - 1, Z_PARTS)
    right = lax.rem(q + 1, Z_PARTS)
    far = lax.rem(q + 2, Z_PARTS)
    factor = learn_rate * 0.2 * math.sqrt(max(rows, cols))
    piece = rows // PIECES

    def owner_at(i):
        return lax.rem(f + i, owners)

    def y_at(i):
        return lax.rem(y + i, y_parts)

    def span(start, size):
        return pl.ds(pl.multiple_of(start * size, size), size)

    loads = [
        pltpu.make_async_copy(momentum, mom_in, load_sem.at[0]),
        pltpu.make_async_copy(weights, mas_in, load_sem.at[1]),
        pltpu.make_async_copy(tokens, tok_in, load_sem.at[2]),
    ]
    for load in loads:
        load.start()

    barrier = pltpu.get_barrier_semaphore()

    @pl.loop(1, owners)
    def _(i):
        pl.semaphore_signal(barrier, inc=1, device_id=(owner_at(i), r), device_id_type=MESH)

    for i in range(1, y_parts):
        pl.semaphore_signal(
            barrier, inc=1, device_id=(f, y_at(i) * Z_PARTS + q), device_id_type=MESH
        )
    for side in (left, right):
        pl.semaphore_signal(
            barrier, inc=1, device_id=(f, y * Z_PARTS + side), device_id_type=MESH
        )

    def local(i):
        return lax.rem(owner_ref[r * owners + i], owners)

    def mom_copy(i):
        return pltpu.make_async_remote_copy(
            src_ref=mom_out.at[i],
            dst_ref=state.at[span(f, shard)],
            send_sem=mom_send.at[i],
            recv_sem=mom_recv.at[i],
            device_id=(owner_at(i), r),
            device_id_type=MESH,
        )

    def mas_copy(i):
        return pltpu.make_async_remote_copy(
            src_ref=mas_out.at[i],
            dst_ref=master.at[span(f, shard)],
            send_sem=mas_send.at[i],
            recv_sem=mas_recv.at[i],
            device_id=(owner_at(i), r),
            device_id_type=MESH,
        )

    def tok_copy(i, k):
        return pltpu.make_async_remote_copy(
            src_ref=tok_out.at[i - 1, k],
            dst_ref=tok_all.at[k, y],
            send_sem=tok_send.at[i - 1, k],
            recv_sem=tok_recv.at[i - 1, k],
            device_id=(f, y_at(i) * Z_PARTS + q),
            device_id_type=MESH,
        )

    def own_copy(c, way):
        return pltpu.make_async_remote_copy(
            src_ref=mats.at[q, span(c, piece)],
            dst_ref=mats.at[q, span(c, piece)],
            send_sem=own_send.at[way, c],
            recv_sem=own_recv.at[way, c],
            device_id=(f, y * Z_PARTS + (right, left)[way]),
            device_id_type=MESH,
        )

    def fwd_copy(j, way):
        held = (left, right)[way]
        c = 2 * j + way
        return pltpu.make_async_remote_copy(
            src_ref=mats.at[held, span(c, piece)],
            dst_ref=mats.at[held, span(c, piece)],
            send_sem=fwd_send.at[way, j],
            recv_sem=fwd_recv.at[way, j],
            device_id=(f, y * Z_PARTS + (right, left)[way]),
            device_id_type=MESH,
        )

    def ans_copy(k, d, j, width, i):
        return pltpu.make_async_remote_copy(
            src_ref=ans_out.at[k, y_at(i), :, span(j, width)],
            dst_ref=answers.at[y * Z_PARTS + k, :, span(j, width)],
            send_sem=ans_send.at[d, j, i - 1],
            recv_sem=ans_recv.at[d, j, i - 1],
            device_id=(f, y_at(i) * Z_PARTS + q),
            device_id_type=MESH,
        )

    loads[0].wait()

    @pl.loop(1, owners)
    def _(i):
        mom_out[i] = mom_in[local(owner_at(i))]

    state[span(f, shard), :] = mom_in[local(f)]
    pl.semaphore_wait(barrier, owners - 1 + y_parts - 1 + 2)

    @pl.loop(1, owners)
    def _(i):
        mom_copy(i).start()

    loads[1].wait()

    @pl.loop(1, owners)
    def _(i):
        mas_out[i] = mas_in[local(owner_at(i))].astype(jnp.bfloat16)
        mas_copy(i).start()

    master[span(f, shard), :] = mas_in[local(f)].astype(jnp.bfloat16)

    loads[2].wait()

    def source(slot):
        found = jnp.int32(0)
        for b in range(blocks):
            found = jnp.where(lax.div(block_ref[b], owners) == slot, b, found)
        return found

    @pl.loop(0, Z_PARTS)
    def _(k):
        for i in range(1, y_parts):
            tok_out[i - 1, k] = tok_in[source(y_at(i) * Z_PARTS + k)]
            tok_copy(i, k).start()
        tok_all[k, y] = tok_in[source(y * Z_PARTS + k)]

    @pl.loop(1, owners)
    def _(i):
        mom_copy(i).wait_recv()

    def squares(i, total):
        wide = state[span(i, shard), :].astype(jnp.float32)
        return total + jnp.sum((wide * wide).reshape(shard // 8, 8, cols), axis=0)

    total = lax.fori_loop(0, owners, squares, jnp.zeros((8, cols), jnp.float32))
    inverse = 1.0 / (jnp.sqrt(jnp.sum(total, keepdims=True)) + norm_eps)

    @pl.loop(0, owners)
    def _(i):
        at = span(i, shard)
        state[at, :] = (state[at, :].astype(jnp.float32) * inverse).astype(jnp.bfloat16)

    def polynomial():
        @pl.loop(0, rows // TILE)
        def _(n):
            square[:, span(n, TILE)] = dot(state[...], state[span(n, TILE), :], True).astype(
                jnp.bfloat16
            )

        @pl.loop(0, rows // TILE)
        def _(n):
            part = square[:, span(n, TILE)]
            poly[:, span(n, TILE)] = (
                quintic_two * part.astype(jnp.float32) + quintic_three * dot(square[...], part)
            ).astype(jnp.bfloat16)

    @pl.loop(0, ITERS - 1)
    def _(step):
        polynomial()

        @pl.loop(0, cols // TILE)
        def _(n):
            part = state[:, span(n, TILE)]
            state[:, span(n, TILE)] = (
                quintic_one * part.astype(jnp.float32) + dot(poly[...], part)
            ).astype(jnp.bfloat16)

    polynomial()

    @pl.loop(1, owners)
    def _(i):
        mas_copy(i).wait_recv()

    @pl.loop(0, rows // TILE)
    def _(m):
        at = span(m, TILE)

        @pl.loop(0, cols // TILE)
        def _(n):
            cut = span(n, TILE)
            update = (
                quintic_one * state[at, cut].astype(jnp.float32)
                + dot(poly[at, :], state[:, cut])
            ).astype(jnp.bfloat16)
            mats[q, at, cut] = (
                master[at, cut].astype(jnp.float32) * (1.0 - learn_rate * weight_decay)
                - factor * update.astype(jnp.float32)
            ).astype(jnp.bfloat16)

        @pl.loop(0, PIECES * TILE // rows)
        def _(c):
            for way in (0, 1):
                own_copy(m * (PIECES * TILE // rows) + c, way).start()

    keep = pltpu.make_async_copy(mats.at[q], fresh.at[0], store_sem.at[0])
    keep.start()

    def relay(first, last):
        @pl.loop(first, last)
        def _(j):
            own_copy(2 * j, 0).wait_recv()
            fwd_copy(j, 0).start()
            own_copy(2 * j, 1).wait_recv()
            own_copy(2 * j + 1, 0).wait_recv()
            own_copy(2 * j + 1, 1).wait_recv()
            fwd_copy(j, 1).start()

    def product(k, d, j, width):
        served = dot(
            tok_all[k].reshape(y_parts * height, cols), mats[k, span(j, width), :], True
        ).astype(jnp.bfloat16)
        ans_out[k, :, :, span(j, width)] = served.reshape(y_parts, height, width)
        answers[y * Z_PARTS + k, :, span(j, width)] = ans_out[k, y, :, span(j, width)]
        for i in range(1, y_parts):
            ans_copy(k, d, j, width, i).start()

    near = rows // TILE
    thin = 2 * piece
    relay(0, PIECES // 4)

    @pl.loop(0, Z_PARTS)
    def _(k):
        for i in range(1, y_parts):
            tok_copy(i, k).wait_recv()

    @pl.loop(0, near)
    def _(j):
        product(q, 0, j, TILE)

    relay(PIECES // 4, PIECES // 2)

    @pl.loop(0, near)
    def _(j):
        product(left, 1, j, TILE)
        product(right, 2, j, TILE)

    @pl.loop(0, PIECES // 2)
    def _(j):
        fwd_copy(j, 0).wait_recv()
        fwd_copy(j, 1).wait_recv()
        product(far, 3, j, thin)

    for i in range(1, y_parts):

        @pl.loop(0, near)
        def _(j):
            for d, k in enumerate((q, left, right)):
                ans_copy(k, d, j, TILE, i).wait_recv()

        @pl.loop(0, PIECES // 2)
        def _(j):
            ans_copy(far, 3, j, thin, i).wait_recv()

    for b in range(blocks):
        result[b * height : (b + 1) * height, :] = answers[lax.div(block_ref[b], owners)]
    leave = pltpu.make_async_copy(result, rollout, store_sem.at[1])
    leave.start()

    @pl.loop(1, owners)
    def _(i):
        mom_copy(i).wait_send()
        mas_copy(i).wait_send()

    for i in range(1, y_parts):

        @pl.loop(0, Z_PARTS)
        def _(k):
            tok_copy(i, k).wait_send()

        @pl.loop(0, near)
        def _(j):
            for d, k in enumerate((q, left, right)):
                ans_copy(k, d, j, TILE, i).wait_send()

        @pl.loop(0, PIECES // 2)
        def _(j):
            ans_copy(far, 3, j, thin, i).wait_send()

    for way in (0, 1):

        @pl.loop(0, PIECES)
        def _(c):
            own_copy(c, way).wait_send()

        @pl.loop(0, PIECES // 2)
        def _(j):
            fwd_copy(j, way).wait_send()

    keep.wait()
    leave.wait()


def per_device(weights, momentum, tokens, block_expert, owner_expert):
    owners = lax.axis_size("fsdp")
    groups = lax.axis_size("replica")
    y_parts = groups // Z_PARTS
    count, shard, cols = momentum.shape
    rows = shard * owners
    blocks = block_expert.shape[0]
    height = tokens.shape[0] // blocks
    half = jnp.bfloat16
    hbm = pl.BlockSpec(memory_space=pl.ANY)
    smem = pl.BlockSpec(memory_space=pltpu.SMEM)
    dma = pltpu.SemaphoreType.DMA
    fresh, rollout = pl.pallas_call(
        kernel,
        name="muon_step",
        out_shape=(
            jax.ShapeDtypeStruct((1, rows, cols), half),
            jax.ShapeDtypeStruct((blocks * height, rows), half),
        ),
        in_specs=[smem, smem, hbm, hbm, hbm],
        out_specs=(hbm, hbm),
        scratch_shapes=[
            pltpu.VMEM((count, shard, cols), half),
            pltpu.VMEM((count, shard, cols), jnp.float32),
            pltpu.VMEM((blocks, height, cols), half),
            pltpu.VMEM((owners, shard, cols), half),
            pltpu.VMEM((owners, shard, cols), half),
            pltpu.VMEM((rows, cols), half),
            pltpu.VMEM((rows, cols), half),
            pltpu.VMEM((y_parts - 1, Z_PARTS, height, cols), half),
            pltpu.VMEM((Z_PARTS, y_parts, height, cols), half),
            pltpu.VMEM((Z_PARTS, rows, cols), half),
            pltpu.VMEM((rows, rows), half),
            pltpu.VMEM((rows, rows), half),
            pltpu.VMEM((Z_PARTS, y_parts, height, rows), half),
            pltpu.VMEM((groups, height, rows), half),
            pltpu.VMEM((blocks * height, rows), half),
            dma((3,)),
            dma((owners,)),
            dma((owners,)),
            dma((owners,)),
            dma((owners,)),
            dma((y_parts - 1, Z_PARTS)),
            dma((y_parts - 1, Z_PARTS)),
            dma((2, PIECES)),
            dma((2, PIECES)),
            dma((2, PIECES // 2)),
            dma((2, PIECES // 2)),
            dma((4, PIECES // 2, y_parts - 1)),
            dma((4, PIECES // 2, y_parts - 1)),
            dma((2,)),
        ],
        compiler_params=pltpu.CompilerParams(
            collective_id=0, has_side_effects=True, vmem_limit_bytes=60 * 2**20
        ),
    )(
        block_expert,
        owner_expert,
        weights,
        momentum,
        tokens.reshape(blocks, height, cols),
    )
    return (fresh, rollout)


def solution(mesh):
    placed = (
        P("replica", "fsdp", None),
        P("replica", "fsdp", None),
        P(("fsdp", "replica"), None),
        P(("fsdp", "replica")),
        P(),
    )
    return jax.shard_map(
        per_device,
        mesh=mesh,
        in_specs=placed,
        out_specs=(P(("fsdp", "replica"), None, None), P(("fsdp", "replica"), None)),
        check_vma=False,
    )
```

```python
import math

import jax
import jax.numpy as jnp
from jax import lax
from jax.experimental import pallas as pl
from jax.experimental.pallas import tpu as pltpu
from jax.sharding import PartitionSpec as P

ITERS = 4
Z_PARTS = 4
PIECES = 8
CORES = 2
PAIR = 2
TILE = 256
WIDE = 512
MESH = pl.DeviceIdType.MESH

quintic_one = 3.4445
quintic_two = -4.775
quintic_three = 2.0315
learn_rate = 0.05
weight_decay = 0.1
norm_eps = 1e-07


def dot(left, right, transposed=False):
    dims = (((1,), (1 if transposed else 0,)), ((), ()))
    return lax.dot_general(left, right, dims, preferred_element_type=jnp.float32)


def kernel(
    block_ref,
    owner_ref,
    weights,
    momentum,
    tokens,
    fresh,
    rollout,
    mom_in,
    mas_in,
    tok_in,
    mom_out,
    mas_out,
    state,
    master,
    tok_out,
    tok_all,
    mats,
    square,
    poly,
    ans_out,
    answers,
    load_sem,
    mom_send,
    mom_recv,
    mas_send,
    mas_recv,
    tok_send,
    tok_recv,
    own_send,
    own_recv,
    fwd_send,
    fwd_recv,
    ans_send,
    ans_recv,
):
    owners = lax.axis_size("fsdp")
    groups = lax.axis_size("replica")
    y_parts = groups // Z_PARTS
    rows, cols = state.shape
    shard = rows // owners
    blocks, height, _ = tok_in.shape
    f = lax.axis_index("fsdp")
    r = lax.axis_index("replica")
    y = r // Z_PARTS
    q = r - y * Z_PARTS
    left = lax.rem(q + Z_PARTS - 1, Z_PARTS)
    right = lax.rem(q + 1, Z_PARTS)
    far = lax.rem(q + 2, Z_PARTS)
    factor = learn_rate * 0.2 * math.sqrt(max(rows, cols))
    piece = rows // PIECES

    inner = PAIR * CORES
    x_parts = owners // inner
    x = f // inner
    z = lax.rem(f // CORES, PAIR)
    core = lax.rem(f, CORES)

    def shift(h):
        return h + h // 2 - 2 * (h // 3)

    def x_from(h):
        return lax.rem(x + x_parts - shift(h), x_parts)

    def chip_from(c):
        return x_from(c // PAIR) * PAIR + lax.rem(z + lax.rem(c, PAIR), PAIR)

    def owner_at(i):
        c = i // CORES
        x_to = lax.rem(x + shift(c // PAIR), x_parts)
        z_to = lax.rem(z + lax.rem(c, PAIR), PAIR)
        return x_to * inner + z_to * CORES + lax.rem(core + lax.rem(i, CORES), CORES)

    def y_at(i):
        return lax.rem(y + i, y_parts)

    def span(start, size):
        return pl.ds(pl.multiple_of(start * size, size), size)

    loads = [
        pltpu.make_async_copy(momentum, mom_in, load_sem.at[0]),
        pltpu.make_async_copy(weights, mas_in, load_sem.at[1]),
        pltpu.make_async_copy(tokens, tok_in, load_sem.at[2]),
    ]
    for load in loads:
        load.start()

    barrier = pltpu.get_barrier_semaphore()

    @pl.loop(1, owners)
    def _(i):
        pl.semaphore_signal(barrier, inc=1, device_id=(owner_at(i), r), device_id_type=MESH)

    for i in range(1, y_parts):
        pl.semaphore_signal(
            barrier, inc=1, device_id=(f, y_at(i) * Z_PARTS + q), device_id_type=MESH
        )
    for side in (left, right):
        pl.semaphore_signal(
            barrier, inc=1, device_id=(f, y * Z_PARTS + side), device_id_type=MESH
        )

    def local(i):
        return lax.rem(owner_ref[r * owners + i], owners)

    def mom_copy(i):
        return pltpu.make_async_remote_copy(
            src_ref=mom_out.at[i],
            dst_ref=state.at[span(f, shard)],
            send_sem=mom_send.at[i],
            recv_sem=mom_recv.at[i],
            device_id=(owner_at(i), r),
            device_id_type=MESH,
        )

    def mas_copy(i):
        return pltpu.make_async_remote_copy(
            src_ref=mas_out.at[i],
            dst_ref=master.at[span(f, shard)],
            send_sem=mas_send.at[i],
            recv_sem=mas_recv.at[i],
            device_id=(owner_at(i), r),
            device_id_type=MESH,
        )

    def tok_copy(i, k):
        return pltpu.make_async_remote_copy(
            src_ref=tok_out.at[i - 1, k],
            dst_ref=tok_all.at[k, y],
            send_sem=tok_send.at[i - 1, k],
            recv_sem=tok_recv.at[i - 1, k],
            device_id=(f, y_at(i) * Z_PARTS + q),
            device_id_type=MESH,
        )

    def own_copy(c, way):
        return pltpu.make_async_remote_copy(
            src_ref=mats.at[q, span(chip_from(c), piece)],
            dst_ref=mats.at[q, span(chip_from(c), piece)],
            send_sem=own_send.at[way, c],
            recv_sem=own_recv.at[way, c],
            device_id=(f, y * Z_PARTS + (right, left)[way]),
            device_id_type=MESH,
        )

    def fwd_copy(j, way):
        held = (left, right)[way]
        c = 2 * j + way
        return pltpu.make_async_remote_copy(
            src_ref=mats.at[held, span(chip_from(c), piece)],
            dst_ref=mats.at[held, span(chip_from(c), piece)],
            send_sem=fwd_send.at[way, j],
            recv_sem=fwd_recv.at[way, j],
            device_id=(f, y * Z_PARTS + (right, left)[way]),
            device_id_type=MESH,
        )

    def ans_copy(k, d, j, width, i, block):
        return pltpu.make_async_remote_copy(
            src_ref=ans_out.at[k, y_at(i), :, span(block, width)],
            dst_ref=answers.at[y * Z_PARTS + k, :, span(block, width)],
            send_sem=ans_send.at[d, j, i - 1],
            recv_sem=ans_recv.at[d, j, i - 1],
            device_id=(f, y_at(i) * Z_PARTS + q),
            device_id_type=MESH,
        )

    loads[0].wait()

    @pl.loop(1, owners)
    def _(i):
        mom_out[i] = mom_in[local(owner_at(i))]

    state[span(f, shard), :] = mom_in[local(f)]
    pl.semaphore_wait(barrier, owners - 1 + y_parts - 1 + 2)

    @pl.loop(1, owners)
    def _(i):
        mom_copy(i).start()

    loads[1].wait()

    @pl.loop(1, owners)
    def _(i):
        mas_out[i] = mas_in[local(owner_at(i))].astype(jnp.bfloat16)
        mas_copy(i).start()

    master[span(f, shard), :] = mas_in[local(f)].astype(jnp.bfloat16)

    loads[2].wait()

    def source(slot):
        found = jnp.int32(0)
        for b in range(blocks):
            found = jnp.where(lax.div(block_ref[b], owners) == slot, b, found)
        return found

    @pl.loop(0, Z_PARTS)
    def _(k):
        for i in range(1, y_parts):
            tok_out[i - 1, k] = tok_in[source(y_at(i) * Z_PARTS + k)]
            tok_copy(i, k).start()
        tok_all[k, y] = tok_in[source(y * Z_PARTS + k)]

    @pl.loop(1, owners)
    def _(i):
        mom_copy(i).wait_recv()

    def squares(i, total):
        wide = state[span(i, shard), :].astype(jnp.float32)
        return total + jnp.sum((wide * wide).reshape(shard // 8, 8, cols), axis=0)

    total = lax.fori_loop(0, owners, squares, jnp.zeros((8, cols), jnp.float32))
    inverse = 1.0 / (jnp.sqrt(jnp.sum(total, keepdims=True)) + norm_eps)

    @pl.loop(0, owners)
    def _(i):
        at = span(i, shard)
        state[at, :] = (state[at, :].astype(jnp.float32) * inverse).astype(jnp.bfloat16)

    tiles = rows // TILE

    @pl.loop(0, ITERS)
    def _(step):
        for n in range(tiles):
            at = slice(n * TILE, (n + 1) * TILE)
            square[:, at] = dot(state[...], state[at, :], True).astype(jnp.bfloat16)
        for n in range(tiles):
            at = slice(n * TILE, (n + 1) * TILE)
            part = square[:, at]
            poly[:, at] = (
                quintic_two * part.astype(jnp.float32) + quintic_three * dot(square[...], part)
            ).astype(jnp.bfloat16)

        @pl.loop(0, cols // WIDE)
        def _(n):
            part = state[:, span(n, WIDE)]
            state[:, span(n, WIDE)] = (
                quintic_one * part.astype(jnp.float32) + dot(poly[...], part)
            ).astype(jnp.bfloat16)

    def finish(c):
        at = span(chip_from(c), piece)
        mats[q, at, :] = (
            master[at, :].astype(jnp.float32) * (1.0 - learn_rate * weight_decay)
            - factor * state[at, :].astype(jnp.float32)
        ).astype(jnp.bfloat16)
        fresh[0, at, :] = mats[q, at, :]
        for way in (0, 1):
            own_copy(c, way).start()

    mas_copy(1).wait_recv()
    finish(0)

    @pl.loop(1, PIECES)
    def _(c):
        for i in range(CORES):
            mas_copy(CORES * c + i).wait_recv()
        finish(c)

    def relay(first, last):
        @pl.loop(first, last)
        def _(j):
            own_copy(2 * j, 0).wait_recv()
            fwd_copy(j, 0).start()
            own_copy(2 * j, 1).wait_recv()
            own_copy(2 * j + 1, 0).wait_recv()
            own_copy(2 * j + 1, 1).wait_recv()
            fwd_copy(j, 1).start()

    def product(k, d, j, width, block):
        served = dot(
            tok_all[k].reshape(y_parts * height, cols), mats[k, span(block, width), :], True
        ).astype(jnp.bfloat16)
        ans_out[k, :, :, span(block, width)] = served.reshape(y_parts, height, width)
        answers[y * Z_PARTS + k, :, span(block, width)] = ans_out[k, y, :, span(block, width)]
        for i in range(1, y_parts):
            ans_copy(k, d, j, width, i, block).start()

    near = rows // TILE
    thin = 2 * piece
    relay(0, PIECES // 4)

    @pl.loop(0, Z_PARTS)
    def _(k):
        for i in range(1, y_parts):
            tok_copy(i, k).wait_recv()

    @pl.loop(0, near)
    def _(j):
        product(q, 0, j, TILE, j)

    relay(PIECES // 4, PIECES // 2)

    @pl.loop(0, near)
    def _(j):
        product(left, 1, j, TILE, j)
        product(right, 2, j, TILE, j)

    @pl.loop(0, PIECES // 2)
    def _(j):
        fwd_copy(j, 0).wait_recv()
        fwd_copy(j, 1).wait_recv()
        product(far, 3, j, thin, x_from(j))

    for i in range(1, y_parts):

        @pl.loop(0, near)
        def _(j):
            for d, k in enumerate((q, left, right)):
                ans_copy(k, d, j, TILE, i, j).wait_recv()

        @pl.loop(0, PIECES // 2)
        def _(j):
            ans_copy(far, 3, j, thin, i, x_from(j)).wait_recv()

    for b in range(blocks):
        rollout[b * height : (b + 1) * height, :] = answers[lax.div(block_ref[b], owners)]

    @pl.loop(1, owners)
    def _(i):
        mom_copy(i).wait_send()
        mas_copy(i).wait_send()

    for i in range(1, y_parts):

        @pl.loop(0, Z_PARTS)
        def _(k):
            tok_copy(i, k).wait_send()

        @pl.loop(0, near)
        def _(j):
            for d, k in enumerate((q, left, right)):
                ans_copy(k, d, j, TILE, i, j).wait_send()

        @pl.loop(0, PIECES // 2)
        def _(j):
            ans_copy(far, 3, j, thin, i, x_from(j)).wait_send()

    for way in (0, 1):

        @pl.loop(0, PIECES)
        def _(c):
            own_copy(c, way).wait_send()

        @pl.loop(0, PIECES // 2)
        def _(j):
            fwd_copy(j, way).wait_send()


def per_device(weights, momentum, tokens, block_expert, owner_expert):
    owners = lax.axis_size("fsdp")
    groups = lax.axis_size("replica")
    y_parts = groups // Z_PARTS
    count, shard, cols = momentum.shape
    rows = shard * owners
    blocks = block_expert.shape[0]
    height = tokens.shape[0] // blocks
    half = jnp.bfloat16
    hbm = pl.BlockSpec(memory_space=pl.ANY)
    vmem = pl.BlockSpec(memory_space=pltpu.VMEM)
    smem = pl.BlockSpec(memory_space=pltpu.SMEM)
    dma = pltpu.SemaphoreType.DMA
    fresh, rollout = pl.pallas_call(
        kernel,
        name="muon_step",
        out_shape=(
            pltpu.VMEM((1, rows, cols), half),
            pltpu.VMEM((blocks * height, rows), half),
        ),
        in_specs=[smem, smem, hbm, hbm, hbm],
        out_specs=(vmem, vmem),
        scratch_shapes=[
            pltpu.VMEM((count, shard, cols), half),
            pltpu.VMEM((count, shard, cols), jnp.float32),
            pltpu.VMEM((blocks, height, cols), half),
            pltpu.VMEM((owners, shard, cols), half),
            pltpu.VMEM((owners, shard, cols), half),
            pltpu.VMEM((rows, cols), half),
            pltpu.VMEM((rows, cols), half),
            pltpu.VMEM((y_parts - 1, Z_PARTS, height, cols), half),
            pltpu.VMEM((Z_PARTS, y_parts, height, cols), half),
            pltpu.VMEM((Z_PARTS, rows, cols), half),
            pltpu.VMEM((rows, rows), half),
            pltpu.VMEM((rows, rows), half),
            pltpu.VMEM((Z_PARTS, y_parts, height, rows), half),
            pltpu.VMEM((groups, height, rows), half),
            dma((3,)),
            dma((owners,)),
            dma((owners,)),
            dma((owners,)),
            dma((owners,)),
            dma((y_parts - 1, Z_PARTS)),
            dma((y_parts - 1, Z_PARTS)),
            dma((2, PIECES)),
            dma((2, PIECES)),
            dma((2, PIECES // 2)),
            dma((2, PIECES // 2)),
            dma((4, PIECES // 2, y_parts - 1)),
            dma((4, PIECES // 2, y_parts - 1)),
        ],
        compiler_params=pltpu.CompilerParams(
            collective_id=0, has_side_effects=True, vmem_limit_bytes=61 * 2**20 - 2**16
        ),
    )(
        block_expert,
        owner_expert,
        weights,
        momentum,
        tokens.reshape(blocks, height, cols),
    )
    return (fresh, rollout)


def solution(mesh):
    placed = (
        P("replica", "fsdp", None),
        P("replica", "fsdp", None),
        P(("fsdp", "replica"), None),
        P(("fsdp", "replica")),
        P(),
    )
    return jax.shard_map(
        per_device,
        mesh=mesh,
        in_specs=placed,
        out_specs=(P(("fsdp", "replica"), None, None), P(("fsdp", "replica"), None)),
        check_vma=False,
    )
```

```python
import math

import jax
import jax.numpy as jnp
from jax import lax
from jax.experimental import pallas as pl
from jax.experimental.pallas import tpu as pltpu
from jax.sharding import PartitionSpec as P

ITERS = 4
Z_PARTS = 4
PIECES = 8
CORES = 2
PAIR = 2
TILE = 256
WIDE = 512
MESH = pl.DeviceIdType.MESH

quintic_one = 3.4445
quintic_two = -4.775
quintic_three = 2.0315
learn_rate = 0.05
weight_decay = 0.1
norm_eps = 1e-07


def dot(left, right, transposed=False):
    dims = (((1,), (1 if transposed else 0,)), ((), ()))
    return lax.dot_general(left, right, dims, preferred_element_type=jnp.float32)


def kernel(
    block_ref,
    owner_ref,
    weights,
    momentum,
    tokens,
    fresh,
    rollout,
    mom_in,
    mas_in,
    tok_in,
    mom_out,
    mas_out,
    state,
    master,
    tok_out,
    tok_all,
    mats,
    square,
    poly,
    ans_out,
    answers,
    load_sem,
    mom_send,
    mom_recv,
    mas_send,
    mas_recv,
    tok_send,
    tok_recv,
    own_send,
    own_recv,
    fwd_send,
    fwd_recv,
    ans_send,
    ans_recv,
):
    owners = lax.axis_size("fsdp")
    groups = lax.axis_size("replica")
    y_parts = groups // Z_PARTS
    rows, cols = state.shape
    shard = rows // owners
    blocks, height, _ = tok_in.shape
    f = lax.axis_index("fsdp")
    r = lax.axis_index("replica")
    y = r // Z_PARTS
    q = r - y * Z_PARTS
    left = lax.rem(q + Z_PARTS - 1, Z_PARTS)
    right = lax.rem(q + 1, Z_PARTS)
    far = lax.rem(q + 2, Z_PARTS)
    factor = learn_rate * 0.2 * math.sqrt(max(rows, cols))
    piece = rows // PIECES

    inner = PAIR * CORES
    x_parts = owners // inner
    x = f // inner
    z = lax.rem(f // CORES, PAIR)
    core = lax.rem(f, CORES)

    def shift(h):
        return h + h // 2 - 2 * (h // 3)

    def x_from(h):
        return lax.rem(x + x_parts - shift(h), x_parts)

    def chip_from(c):
        return x_from(lax.rem(c, x_parts)) * PAIR + lax.rem(z + c // x_parts, PAIR)

    def owner_at(i):
        c = i // CORES
        x_to = lax.rem(x + shift(lax.rem(c, x_parts)), x_parts)
        z_to = lax.rem(z + c // x_parts, PAIR)
        return x_to * inner + z_to * CORES + lax.rem(core + lax.rem(i, CORES), CORES)

    def y_at(i):
        return lax.rem(y + i, y_parts)

    def span(start, size):
        return pl.ds(pl.multiple_of(start * size, size), size)

    loads = [
        pltpu.make_async_copy(momentum, mom_in, load_sem.at[0]),
        pltpu.make_async_copy(weights, mas_in, load_sem.at[1]),
        pltpu.make_async_copy(tokens, tok_in, load_sem.at[2]),
    ]
    for load in loads:
        load.start()

    barrier = pltpu.get_barrier_semaphore()

    @pl.loop(1, owners)
    def _(i):
        pl.semaphore_signal(barrier, inc=1, device_id=(owner_at(i), r), device_id_type=MESH)

    for i in range(1, y_parts):
        pl.semaphore_signal(
            barrier, inc=1, device_id=(f, y_at(i) * Z_PARTS + q), device_id_type=MESH
        )
    for side in (left, right):
        pl.semaphore_signal(
            barrier, inc=1, device_id=(f, y * Z_PARTS + side), device_id_type=MESH
        )

    def local(i):
        return lax.rem(owner_ref[r * owners + i], owners)

    def mom_copy(i):
        return pltpu.make_async_remote_copy(
            src_ref=mom_out.at[i],
            dst_ref=state.at[span(f, shard)],
            send_sem=mom_send.at[i],
            recv_sem=mom_recv.at[i],
            device_id=(owner_at(i), r),
            device_id_type=MESH,
        )

    def mas_copy(i):
        return pltpu.make_async_remote_copy(
            src_ref=mas_out.at[i],
            dst_ref=master.at[span(f, shard)],
            send_sem=mas_send.at[i],
            recv_sem=mas_recv.at[i],
            device_id=(owner_at(i), r),
            device_id_type=MESH,
        )

    def tok_copy(i, k):
        return pltpu.make_async_remote_copy(
            src_ref=tok_out.at[i - 1, k],
            dst_ref=tok_all.at[k, y],
            send_sem=tok_send.at[i - 1, k],
            recv_sem=tok_recv.at[i - 1, k],
            device_id=(f, y_at(i) * Z_PARTS + q),
            device_id_type=MESH,
        )

    def own_copy(c, way):
        return pltpu.make_async_remote_copy(
            src_ref=mats.at[q, span(chip_from(c), piece)],
            dst_ref=mats.at[q, span(chip_from(c), piece)],
            send_sem=own_send.at[way, c],
            recv_sem=own_recv.at[way, c],
            device_id=(f, y * Z_PARTS + (right, left)[way]),
            device_id_type=MESH,
        )

    def fwd_copy(j, way):
        held = (left, right)[way]
        c = j + way * (PIECES // 2)
        return pltpu.make_async_remote_copy(
            src_ref=mats.at[held, span(chip_from(c), piece)],
            dst_ref=mats.at[held, span(chip_from(c), piece)],
            send_sem=fwd_send.at[way, j],
            recv_sem=fwd_recv.at[way, j],
            device_id=(f, y * Z_PARTS + (right, left)[way]),
            device_id_type=MESH,
        )

    def ans_copy(k, d, j, width, i, block):
        return pltpu.make_async_remote_copy(
            src_ref=ans_out.at[k, y_at(i), :, span(block, width)],
            dst_ref=answers.at[y * Z_PARTS + k, :, span(block, width)],
            send_sem=ans_send.at[d, j, i - 1],
            recv_sem=ans_recv.at[d, j, i - 1],
            device_id=(f, y_at(i) * Z_PARTS + q),
            device_id_type=MESH,
        )

    loads[0].wait()

    @pl.loop(1, owners)
    def _(i):
        mom_out[i] = mom_in[local(owner_at(i))]

    state[span(f, shard), :] = mom_in[local(f)]
    pl.semaphore_wait(barrier, owners - 1 + y_parts - 1 + 2)

    @pl.loop(1, owners)
    def _(i):
        mom_copy(i).start()

    loads[1].wait()

    @pl.loop(1, owners)
    def _(i):
        mas_out[i] = mas_in[local(owner_at(i))].astype(jnp.bfloat16)
        mas_copy(i).start()

    master[span(f, shard), :] = mas_in[local(f)].astype(jnp.bfloat16)

    loads[2].wait()

    def source(slot):
        found = jnp.int32(0)
        for b in range(blocks):
            found = jnp.where(lax.div(block_ref[b], owners) == slot, b, found)
        return found

    @pl.loop(0, Z_PARTS)
    def _(k):
        for i in range(1, y_parts):
            tok_out[i - 1, k] = tok_in[source(y_at(i) * Z_PARTS + k)]
            tok_copy(i, k).start()
        tok_all[k, y] = tok_in[source(y * Z_PARTS + k)]

    @pl.loop(1, owners)
    def _(i):
        mom_copy(i).wait_recv()

    def squares(i, total):
        wide = state[span(i, shard), :].astype(jnp.float32)
        return total + jnp.sum((wide * wide).reshape(shard // 8, 8, cols), axis=0)

    total = lax.fori_loop(0, owners, squares, jnp.zeros((8, cols), jnp.float32))
    inverse = 1.0 / (jnp.sqrt(jnp.sum(total, keepdims=True)) + norm_eps)

    @pl.loop(0, owners)
    def _(i):
        at = span(i, shard)
        state[at, :] = (state[at, :].astype(jnp.float32) * inverse).astype(jnp.bfloat16)

    tiles = rows // TILE

    @pl.loop(0, ITERS)
    def _(step):
        for n in range(tiles):
            at = slice(n * TILE, (n + 1) * TILE)
            square[:, at] = dot(state[...], state[at, :], True).astype(jnp.bfloat16)
        for n in range(tiles):
            at = slice(n * TILE, (n + 1) * TILE)
            part = square[:, at]
            poly[:, at] = (
                quintic_two * part.astype(jnp.float32) + quintic_three * dot(square[...], part)
            ).astype(jnp.bfloat16)

        @pl.loop(0, cols // WIDE)
        def _(n):
            part = state[:, span(n, WIDE)]
            state[:, span(n, WIDE)] = (
                quintic_one * part.astype(jnp.float32) + dot(poly[...], part)
            ).astype(jnp.bfloat16)

    def finish(c):
        at = span(chip_from(c), piece)
        mats[q, at, :] = (
            master[at, :].astype(jnp.float32) * (1.0 - learn_rate * weight_decay)
            - factor * state[at, :].astype(jnp.float32)
        ).astype(jnp.bfloat16)
        fresh[0, at, :] = mats[q, at, :]
        for way in (0, 1):
            own_copy(c, way).start()

    mas_copy(1).wait_recv()
    finish(0)

    @pl.loop(1, PIECES)
    def _(c):
        for i in range(CORES):
            mas_copy(CORES * c + i).wait_recv()
        finish(c)

    def relay(way):
        @pl.loop(0, PIECES // 2)
        def _(j):
            for side in (0, 1):
                own_copy(j + way * (PIECES // 2), side).wait_recv()
            fwd_copy(j, way).start()

    def product(k, d, j, width, block):
        served = dot(
            tok_all[k].reshape(y_parts * height, cols), mats[k, span(block, width), :], True
        ).astype(jnp.bfloat16)
        ans_out[k, :, :, span(block, width)] = served.reshape(y_parts, height, width)
        answers[y * Z_PARTS + k, :, span(block, width)] = ans_out[k, y, :, span(block, width)]
        for i in range(1, y_parts):
            ans_copy(k, d, j, width, i, block).start()

    near = rows // TILE
    thin = 2 * piece
    relay(0)

    @pl.loop(0, Z_PARTS)
    def _(k):
        for i in range(1, y_parts):
            tok_copy(i, k).wait_recv()

    @pl.loop(0, near)
    def _(j):
        product(q, 0, j, TILE, j)

    relay(1)

    @pl.loop(0, near)
    def _(j):
        product(left, 1, j, TILE, j)
        product(right, 2, j, TILE, j)

    def serve_far(j):
        for way in (0, 1):
            fwd_copy(j, way).wait_recv()
        product(far, 3, j, thin, x_from(j))

    last = PIECES // 2 - 1

    @pl.loop(0, last)
    def _(j):
        serve_far(j)

    @pl.loop(1, owners)
    def _(i):
        mom_copy(i).wait_send()
        mas_copy(i).wait_send()

    for i in range(1, y_parts):

        @pl.loop(0, Z_PARTS)
        def _(k):
            tok_copy(i, k).wait_send()

        @pl.loop(0, near)
        def _(j):
            for d, k in enumerate((q, left, right)):
                ans_copy(k, d, j, TILE, i, j).wait()

    for way in (0, 1):

        @pl.loop(0, PIECES)
        def _(c):
            own_copy(c, way).wait_send()

    serve_far(last)

    for i in range(1, y_parts):

        @pl.loop(0, PIECES // 2)
        def _(j):
            ans_copy(far, 3, j, thin, i, x_from(j)).wait_recv()

    for b in range(blocks):
        rollout[b * height : (b + 1) * height, :] = answers[lax.div(block_ref[b], owners)]

    for i in range(1, y_parts):

        @pl.loop(0, PIECES // 2)
        def _(j):
            ans_copy(far, 3, j, thin, i, x_from(j)).wait_send()

    for way in (0, 1):

        @pl.loop(0, PIECES // 2)
        def _(j):
            fwd_copy(j, way).wait_send()


def per_device(weights, momentum, tokens, block_expert, owner_expert):
    owners = lax.axis_size("fsdp")
    groups = lax.axis_size("replica")
    y_parts = groups // Z_PARTS
    count, shard, cols = momentum.shape
    rows = shard * owners
    blocks = block_expert.shape[0]
    height = tokens.shape[0] // blocks
    half = jnp.bfloat16
    hbm = pl.BlockSpec(memory_space=pl.ANY)
    vmem = pl.BlockSpec(memory_space=pltpu.VMEM)
    smem = pl.BlockSpec(memory_space=pltpu.SMEM)
    dma = pltpu.SemaphoreType.DMA
    fresh, rollout = pl.pallas_call(
        kernel,
        name="muon_step",
        out_shape=(
            pltpu.VMEM((1, rows, cols), half),
            pltpu.VMEM((blocks * height, rows), half),
        ),
        in_specs=[smem, smem, hbm, hbm, hbm],
        out_specs=(vmem, vmem),
        scratch_shapes=[
            pltpu.VMEM((count, shard, cols), half),
            pltpu.VMEM((count, shard, cols), jnp.float32),
            pltpu.VMEM((blocks, height, cols), half),
            pltpu.VMEM((owners, shard, cols), half),
            pltpu.VMEM((owners, shard, cols), half),
            pltpu.VMEM((rows, cols), half),
            pltpu.VMEM((rows, cols), half),
            pltpu.VMEM((y_parts - 1, Z_PARTS, height, cols), half),
            pltpu.VMEM((Z_PARTS, y_parts, height, cols), half),
            pltpu.VMEM((Z_PARTS, rows, cols), half),
            pltpu.VMEM((rows, rows), half),
            pltpu.VMEM((rows, rows), half),
            pltpu.VMEM((Z_PARTS, y_parts, height, rows), half),
            pltpu.VMEM((groups, height, rows), half),
            dma((3,)),
            dma((owners,)),
            dma((owners,)),
            dma((owners,)),
            dma((owners,)),
            dma((y_parts - 1, Z_PARTS)),
            dma((y_parts - 1, Z_PARTS)),
            dma((2, PIECES)),
            dma((2, PIECES)),
            dma((2, PIECES // 2)),
            dma((2, PIECES // 2)),
            dma((4, PIECES // 2, y_parts - 1)),
            dma((4, PIECES // 2, y_parts - 1)),
        ],
        compiler_params=pltpu.CompilerParams(
            collective_id=0, has_side_effects=True, vmem_limit_bytes=61 * 2**20 - 2**16
        ),
    )(
        block_expert,
        owner_expert,
        weights,
        momentum,
        tokens.reshape(blocks, height, cols),
    )
    return (fresh, rollout)


def solution(mesh):
    placed = (
        P("replica", "fsdp", None),
        P("replica", "fsdp", None),
        P(("fsdp", "replica"), None),
        P(("fsdp", "replica")),
        P(),
    )
    return jax.shard_map(
        per_device,
        mesh=mesh,
        in_specs=placed,
        out_specs=(P(("fsdp", "replica"), None, None), P(("fsdp", "replica"), None)),
        check_vma=False,
    )
```
